32 devices in a mesh: tm: 2 (over y), space: 16 (over z, x, core).
Axes of the slice: x: 2, y: 2, z: 4, core: 2. Of those that a mesh axis runs over, the one named last changes fastest.
Arguments:
- noisy_state: float32 [8, 2, 256, 256], P('tm', None, 'space'), may hold values from -6 to 6
- fresh_noise: float32 [8, 2, 256, 256], P('tm', None, 'space'), may hold values from -6 to 6
- level_index: int32 [1], replicated, may hold values from 1 to 31
- station_obs: float32 [8, 2, 2048], P('tm', None, 'space'), may hold values from -6 to 6
- obs_variance: float32 [2048], P('space'), may hold values from 0.05 to 0.5
- station_owner: int32 [2048, 1], P('space'), may hold values from 0 to 15; in each aligned block of 128 rows (0 to 127, 128 to 255, ...) at most 32 rows name the same one
- station_cell: int32 [2048], P('space'), may hold values from 0 to 4095
- conv_in: bfloat16 [3, 64, 48], replicated, may hold values from -0.5 to 0.5
- conv_mid: bfloat16 [3, 64, 192], replicated, may hold values from -0.25 to 0.25
- conv_res: bfloat16 [3, 64, 192], replicated, may hold values from -0.25 to 0.25
- conv_out: bfloat16 [3, 16, 192], replicated, may hold values from -0.25 to 0.25
- in_bias: float32 [64], replicated, may hold values from -3 to 3
- noise_embed: float32 [64], replicated, may hold values from -3 to 3
- norm_gain: float32 [64], replicated, may hold values from 0.5 to 2
Outputs:
- next_state: float32 [8, 2, 256, 256], P('tm', None, 'space')
The draws below stay inside these ranges and needn't reach their ends.
Inputs may be any that keep to these rules, and one draw needn't show every extreme that they name: `station_owner`: among the stations of one device (each aligned block of 128 stations) at most 32 have the same owner strip; every strip owns some station.
All inputs are finite; a program needn't handle non-finite values.
Results may differ from the reference program's by a relative error of at most 0.0023.
Values may be sent and summed in bfloat16 or wider, within the bound.
A program may use at most 64 MiB of HBM per device.

```python
import math
import jax
import jax.numpy as jnp
import numpy as np
from jax import lax

C = 64
WIN = 8
LEVELS = 32
ROWS = 16
COLS = 256
STA_DEV = 128
STRIDE = 4
CHAN = 16
TIMES = 8
NY = 256
NX = 256
STATIONS = 2048
CAP = 32
N_SPACE = 16


def plant(values, stream_key, least, high):
    longest = values.shape.index(max(values.shape))
    spots = []
    for shift in (0, 1):
        where = [jax.random.randint(jax.random.fold_in(stream_key, axis), (), 0, length) for axis, length in enumerate(values.shape)]
        where[longest] = (where[longest] + shift) % values.shape[longest]
        spots.append(tuple(where))
    return values.at[spots[0]].set(least).at[spots[1]].set(high)


def block_levels(stream_key, extent, pieces, least, top_value):
    level, own = 1.0, jax.random.fold_in(stream_key, 6)
    for axis_at, shards_of in pieces:
        draws = jnp.exp(jax.random.uniform(jax.random.fold_in(own, axis_at), (shards_of,), jnp.float32, least / len(pieces), top_value / len(pieces)))
        level = level * jnp.repeat(draws, extent[axis_at] // shards_of).reshape([-1 if axis == axis_at else 1 for axis in range(len(extent))])
    return level


def routed_block(key, own, number, rows, amount, top, bound, skew):
    order = jax.random.permutation(key, amount)
    packed, usual = portions_of(amount, rows * top, bound, skew, True), portions_of(amount, rows * top, bound, skew, False)
    places = jnp.arange(amount)

    def named(sizes, turn):
        used = int((sizes > 0).sum())
        fixed = max(1, used // 4)
        shifted = fixed + (places - fixed + turn * (used - fixed)) % max(1, amount - fixed)
        return jnp.zeros((amount,), jnp.int32).at[order[jnp.where(places < fixed, places, shifted)]].set(jnp.asarray(sizes, jnp.int32))

    sizes = jnp.where(number % 4 == 0, named(packed, number // 4), named(usual, number - number // 4 - 1))
    mixed = jax.random.permutation(jax.random.fold_in(own, 3), amount)
    donor, taker = mixed[0:amount // 2 * 2:2], mixed[1:amount // 2 * 2:2]
    room = jnp.minimum(sizes[donor] - 1, bound - sizes[taker]) // 2
    room = jnp.where((donor == order[0]) | (taker == order[0]) | (sizes[taker] == 0), 0, jnp.maximum(room, 0))
    shifted = jax.random.randint(jax.random.fold_in(own, 4), (amount // 2,), 0, 1 << 20) % (room + 1)
    sizes = sizes.at[donor].add(-shifted).at[taker].add(shifted)
    items = jnp.searchsorted(jnp.cumsum(sizes), jnp.arange(rows * top), side="right").astype(jnp.int32)
    listing = items.reshape(top, rows).T
    listing = listing[jax.random.permutation(jax.random.fold_in(own, 1), rows)]
    turn = jax.random.randint(jax.random.fold_in(own, 2), (rows, 1), 0, top)
    return jnp.take_along_axis(listing, (jnp.arange(top)[None, :] + turn) % top, axis=1)


def portions_of(count, total, bound, skew, full):
    weights = [(1 << 20) // math.isqrt(grade ** skew) + 1 for grade in range(1, count + 1)]
    largest = bound if full else min(bound, max(-(-total // count), total * weights[0] // sum(weights)))
    least = 1 if total - largest >= count - 1 else 0
    holding, rest = [largest] + [least] * (count - 1), total - largest - least * (count - 1)
    while rest > 0:
        movable = [i for i in range(1, count) if holding[i] < largest] or [i for i in range(1, count) if holding[i] < bound]
        mass, left = sum([weights[i] for i in movable]), rest
        for i in movable:
            addition = min(bound - holding[i], max(1, left * weights[i] // mass), rest)
            holding[i] = holding[i] + addition
            rest = rest - addition
    return np.array(holding)


def normal_values(key, extent, deviation, limit, shards=(), held_as=jnp.bfloat16):
    values = jax.random.normal(key, extent, jnp.float32) * deviation
    if len(shards) > 0:
        values = block_levels(key, extent, shards, -0.22, 0.18) * values
    return jnp.clip(values, min=-limit, max=limit).astype(held_as)


def setup_inputs(seed: int = 0) -> dict:
    splits = jax.random.split(jax.random.key(seed), 15)
    noisy_state = normal_values(splits[0], (TIMES, 2, NY, NX), 1.0, 6.0, ((0, 2), (2, 16)), jnp.float32)
    fresh_noise = normal_values(splits[1], (TIMES, 2, NY, NX), 1.0, 6.0, ((0, 2), (2, 16)), jnp.float32)
    level_index = jax.random.randint(splits[2], (1,), 1, LEVELS).astype(jnp.int32)
    station_obs = normal_values(splits[3], (TIMES, 2, STATIONS), 1.0, 6.0, ((0, 2), (2, 16)), jnp.float32)
    obs_variance = jnp.clip(jnp.exp(math.log(0.5) - 2.3025851 * jax.random.uniform(splits[4], (STATIONS,), jnp.float32) ** block_levels(splits[4], (STATIONS,), ((0, 16),), -0.2, 0.2)), 0.05, 0.5)
    station_owner_keys = jax.random.split(jax.random.fold_in(splits[5], 1), STATIONS // STA_DEV)
    station_owner_turns = jax.random.permutation(jax.random.fold_in(splits[5], 3), STATIONS // STA_DEV)
    station_owner = jax.vmap(lambda own, number: routed_block(jax.random.fold_in(splits[5], 2), own, number, STA_DEV, N_SPACE, 1, CAP, 2))(station_owner_keys, station_owner_turns).reshape((STATIONS, 1))
    station_cell = plant(jax.random.randint(splits[6], (STATIONS,), 0, ROWS * COLS), jax.random.fold_in(splits[6], 1), 0, (ROWS * COLS) - 1).astype(jnp.int32)
    conv_in = normal_values(splits[7], (3, C, 3 * CHAN), (9 * CHAN) ** -0.5, 0.5)
    conv_mid = normal_values(splits[8], (3, C, 3 * C), (9 * C) ** -0.5, 0.25)
    conv_res = normal_values(splits[9], (3, C, 3 * C), (9 * C) ** -0.5, 0.25)
    conv_out = normal_values(splits[10], (3, CHAN, 3 * C), (9 * C) ** -0.5, 0.25)
    in_bias = normal_values(splits[11], (C,), 0.5, 3.0, (), jnp.float32)
    noise_embed = normal_values(splits[12], (C,), 0.5, 3.0, (), jnp.float32)
    norm_gain = jnp.clip(jnp.exp(jax.random.uniform(splits[13], (C,), jnp.float32, math.log(0.5), math.log(2.0))), 0.5, 2.0)
    return dict(noisy_state=noisy_state, fresh_noise=fresh_noise, level_index=level_index, station_obs=station_obs, obs_variance=obs_variance, station_owner=station_owner, station_cell=station_cell, conv_in=conv_in, conv_mid=conv_mid, conv_res=conv_res, conv_out=conv_out, in_bias=in_bias, noise_embed=noise_embed, norm_gain=norm_gain)


def scale_at(level):
    return 0.3 * jnp.exp(jnp.log(5.0) * level.astype(jnp.float32) / (LEVELS - 1))

def conv_full(weight, field):
    inputs = field.shape[0]
    moving = field.astype(jnp.float32)
    total = jnp.zeros((weight.shape[1],) + field.shape[1:], jnp.float32)
    for row_tap in range(3):
        for col_tap in range(3):
            moved = jnp.roll(moving, (1 - row_tap, 1 - col_tap), axis=(1, 2))
            kernel = weight[row_tap][:, col_tap * inputs:(col_tap + 1) * inputs].astype(jnp.float32)
            total = total + jnp.einsum('oc,cyx->oyx', kernel, moved)
    return total

def score_full(window_in, conv_in, conv_mid, conv_res, conv_out, bias, norm_gain):
    first = jax.nn.silu(conv_full(conv_in, window_in) + bias[:, None, None]).astype(jnp.bfloat16)
    middle = conv_full(conv_mid, first)
    normed = middle * lax.rsqrt(lax.optimization_barrier(jnp.mean(middle * middle, axis=0, keepdims=True)) + 1e-05) * norm_gain[:, None, None]
    second = jax.nn.silu(normed).astype(jnp.bfloat16)
    branch = jax.nn.silu(conv_full(conv_res, second))
    third = (first.astype(jnp.float32) + branch).astype(jnp.bfloat16)
    return conv_full(conv_out, third)

def reference(noisy_state, fresh_noise, level_index, station_obs, obs_variance, station_owner, station_cell, conv_in, conv_mid, conv_res, conv_out, in_bias, noise_embed, norm_gain):
    noise_scale = scale_at(level_index[0])
    next_scale = scale_at(level_index[0] - 1)
    bias = in_bias + noise_embed * jnp.log(10.0 * noise_scale)
    scaled = (noisy_state / jnp.sqrt(1.0 + noise_scale * noise_scale)).astype(jnp.bfloat16)
    window_total = TIMES // STRIDE - 1

    def accumulate(summed, window):
        start_step = (window * STRIDE).astype(jnp.int32)
        window_in = lax.dynamic_slice_in_dim(scaled, start_step, WIN, 0).reshape(CHAN, NY, NX)
        result = score_full(window_in, conv_in, conv_mid, conv_res, conv_out, bias, norm_gain).reshape(WIN, 2, NY, NX)
        current = lax.dynamic_slice_in_dim(summed, start_step, WIN, 0)
        return (lax.dynamic_update_slice_in_dim(summed, current + result, start_step, 0), None)
    summed, unused = lax.scan(accumulate, jnp.zeros((TIMES, 2, NY, NX), jnp.float32), jnp.arange(window_total, dtype=jnp.int32))
    moment = jnp.arange(TIMES, dtype=jnp.int32)
    cover = jnp.where((moment < STRIDE) | (moment >= TIMES - STRIDE), 1.0, 2.0).astype(jnp.float32)
    estimate = noisy_state - noise_scale * (summed / cover[:, None, None, None])
    owners = station_owner[:, 0]
    row_of = (owners * ROWS + station_cell // COLS).astype(jnp.int32)
    col_of = (station_cell % COLS).astype(jnp.int32)
    seen = estimate[:, :, row_of, col_of]
    misfit = (station_obs - seen) / (obs_variance + noise_scale * noise_scale)
    pull = jnp.zeros_like(estimate).at[:, :, row_of, col_of].add(misfit)
    return estimate + noise_scale * noise_scale * pull + next_scale * fresh_noise
```

```python
import jax
import jax.numpy as jnp
from jax import lax
from jax.experimental import pallas as pl
from jax.experimental.pallas import tpu as pltpu
from jax.sharding import PartitionSpec as P

WIN = 8
LEVELS = 32
STRIDE = 4
CHAN = 16


def extended_2(cells, sides, width):
    for axis, dim in sides:
        count = lax.axis_size(axis)
        head = lax.slice_in_dim(cells, 0, width, axis=dim)
        tail = lax.slice_in_dim(cells, cells.shape[dim] - width, cells.shape[dim], axis=dim)
        cells = jnp.concatenate(
            [
                lax.ppermute(tail, axis, [(i, (i + 1) % count) for i in range(count)]),
                cells,
                lax.ppermute(head, axis, [((i + 1) % count, i) for i in range(count)]),
            ],
            axis=dim,
        )
    return cells


def shifted(value, axis, steps):
    count = lax.axis_size(axis)
    first, last = (max(0, -steps), min(count, count - steps))
    return lax.ppermute(value, axis, [(source, source + steps) for source in range(first, last)])


def scale_at(level):
    return 0.3 * jnp.exp(jnp.log(5.0) * level.astype(jnp.float32) / (LEVELS - 1))


def conv_rows(weight, padded):
    out_rows = padded.shape[2] - 2
    stacked = jnp.concatenate(
        [jnp.roll(padded, 1 - col_tap, axis=3) for col_tap in range(3)], axis=1
    )
    total = None
    for row_tap in range(3):
        product = jnp.einsum(
            "oc,ncyx->noyx",
            weight[row_tap],
            stacked[:, :, row_tap : row_tap + out_rows, :],
            preferred_element_type=jnp.float32,
        )
        total = product if total is None else total + product
    return total


def hidden_rim(hidden):
    return extended_2(hidden, (("space", 2),), 1)


def score_net(windows, conv_in, conv_mid, conv_res, conv_out, bias, norm_gain):
    source = extended_2(windows, (("space", 2),), 1)
    first = jax.nn.silu(conv_rows(conv_in, source) + bias[None, :, None, None]).astype(jnp.bfloat16)
    middle = conv_rows(conv_mid, hidden_rim(first))
    normed = (
        middle
        * lax.rsqrt(jnp.mean(middle * middle, axis=1, keepdims=True) + 1e-05)
        * norm_gain[None, :, None, None]
    )
    second = jax.nn.silu(normed).astype(jnp.bfloat16)
    branch = jax.nn.silu(conv_rows(conv_res, hidden_rim(second)))
    third = (first.astype(jnp.float32) + branch).astype(jnp.bfloat16)
    return conv_rows(conv_out, hidden_rim(third))


def local(
    noisy_state,
    fresh_noise,
    level_index,
    station_obs,
    obs_variance,
    station_owner,
    station_cell,
    conv_in,
    conv_mid,
    conv_res,
    conv_out,
    in_bias,
    noise_embed,
    norm_gain,
):
    step_count, layer_count, row_count, col_count = noisy_state.shape
    noise_scale = scale_at(level_index[0])
    next_scale = scale_at(level_index[0] - 1)
    bias = in_bias + noise_embed * jnp.log(10.0 * noise_scale)
    scaled = (noisy_state / jnp.sqrt(1.0 + noise_scale * noise_scale)).astype(jnp.bfloat16)
    time_rank = lax.axis_index("tm")
    total_steps = step_count * lax.axis_size("tm")
    ahead = shifted(scaled, "tm", -1)
    extended = jnp.concatenate([scaled, ahead], axis=0)
    offset = 0
    window_count = (extended.shape[0] - WIN) // STRIDE + 1
    windows = jnp.stack([extended])
    windows = windows.reshape(window_count, CHAN, row_count, col_count)
    outputs = score_net(windows, conv_in, conv_mid, conv_res, conv_out, bias, norm_gain)
    starts = time_rank * step_count - offset + STRIDE * jnp.arange(window_count, dtype=jnp.int32)
    usable = ((starts >= 0) & (starts + WIN <= total_steps)).astype(jnp.float32)
    halves = (
        outputs.reshape(window_count, 2, STRIDE, layer_count, row_count, col_count)
        * usable[:, None, None, None, None, None]
    )
    blank = jnp.zeros((1, STRIDE, layer_count, row_count, col_count), jnp.float32)
    summed = jnp.concatenate([halves[:, 0], blank], axis=0) + jnp.concatenate(
        [blank, halves[:, 1]], axis=0
    )
    summed = summed.reshape(extended.shape[0], layer_count, row_count, col_count)
    spill = shifted(summed[step_count:], "tm", 1)
    own = jnp.concatenate([summed[:STRIDE] + spill, summed[STRIDE:step_count]], axis=0)
    moment = time_rank * step_count + jnp.arange(step_count, dtype=jnp.int32)
    cover = jnp.where((moment < STRIDE) | (moment >= total_steps - STRIDE), 1.0, 2.0).astype(
        jnp.float32
    )
    estimate = noisy_state - noise_scale * (own / cover[:, None, None, None])
    space_size = lax.axis_size("space")
    station_count = station_cell.shape[0]
    capacity = 4 * station_count // space_size
    values = station_obs.reshape(step_count * layer_count, station_count)
    target = station_owner[:, 0]
    earlier = lax.broadcasted_iota(
        jnp.int32, (station_count, station_count), 0
    ) < lax.broadcasted_iota(jnp.int32, (station_count, station_count), 1)
    ranked = jnp.sum(
        jnp.where((target[:, None] == target[None, :]) & earlier, 1, 0), axis=0
    ).astype(jnp.int32)
    slot = target * capacity + ranked
    slot_count = space_size * capacity
    value_slots = jnp.zeros((values.shape[0], slot_count), jnp.float32).at[:, slot].set(values)
    spread_slots = jnp.zeros((1, slot_count), jnp.float32).at[0, slot].set(obs_variance)
    cell_slots = jnp.full((1, slot_count), -1, jnp.int32).at[0, slot].set(station_cell)
    got_values, got_spread, got_cells = (
        lax.all_to_all(value_slots, "space", split_axis=1, concat_axis=1, tiled=True),
        lax.all_to_all(spread_slots, "space", split_axis=1, concat_axis=1, tiled=True),
        lax.all_to_all(cell_slots, "space", split_axis=1, concat_axis=1, tiled=True),
    )
    present = got_cells[0] >= 0
    spot = jnp.maximum(got_cells[0], 0)
    flat = estimate.reshape(step_count * layer_count, row_count * col_count)
    seen = jnp.take(flat, spot, axis=1)
    misfit = jnp.where(
        present[None, :], (got_values - seen) / (got_spread + noise_scale * noise_scale), 0.0
    )
    pull = jnp.zeros_like(flat).at[:, spot].add(misfit)
    return (
        estimate
        + noise_scale * noise_scale * pull.reshape(estimate.shape)
        + next_scale * fresh_noise
    )


MESH = pl.DeviceIdType.MESH
HALO = 4


def gate(v):
    return 0.5 * v * (jnp.tanh(0.5 * v) + 1.0)


def with_neighbours(v):
    cols = v.shape[1]
    return jnp.concatenate(
        [pltpu.roll(v, 1, axis=1), v, pltpu.roll(v, cols - 1, axis=1)], axis=0
    ).astype(jnp.bfloat16)


def fused_kernel(
    space,
    scaled_ref,
    pack_ref,
    w_in_ref,
    w_mid_ref,
    w_res_ref,
    w_out_ref,
    bias_ref,
    gain_ref,
    den_ref,
    pull_ref,
    win,
    sta,
    cols_in,
    cols_hid,
    cols_sec,
    cols_third,
    prod,
    first,
    result,
    arrived,
    left_hand,
    right_hand,
    send_halo,
    recv_halo,
    send_sta,
    recv_sta,
    send_out,
    recv_out,
):
    t = lax.axis_index("tm")
    s = lax.axis_index("space")
    peer = 1 - t
    after = lax.rem(s + 1, space)
    before = lax.rem(s + space - 1, space)
    diagonal = lax.rem(s + space - 1 + 2 * t, space)
    strip = scaled_ref.shape[0]
    half = strip // 2
    span = half + HALO
    chans = scaled_ref.shape[1]
    hidden = bias_ref.shape[0]
    width = scaled_ref.shape[2]

    barrier = pltpu.get_barrier_semaphore()
    pl.semaphore_signal(barrier, inc=1, device_id=(peer, s), device_id_type=MESH)
    pl.semaphore_signal(barrier, inc=1, device_id=(peer, diagonal), device_id_type=MESH)
    for d in range(1, space):
        pl.semaphore_signal(
            barrier, inc=1, device_id=(t, lax.rem(s + d, space)), device_id_type=MESH
        )
    pl.semaphore_wait(barrier, space + 1)

    to_peer = pltpu.make_async_remote_copy(
        src_ref=scaled_ref.at[pl.ds(HALO * peer, span)],
        dst_ref=win.at[t, pl.ds(HALO * t, span)],
        send_sem=send_halo.at[0],
        recv_sem=recv_halo.at[0],
        device_id=(peer, s),
        device_id_type=MESH,
    )
    to_after = pltpu.make_async_remote_copy(
        src_ref=scaled_ref.at[pl.ds(strip - HALO, HALO)],
        dst_ref=win.at[t, pl.ds(0, HALO)],
        send_sem=send_halo.at[1],
        recv_sem=recv_halo.at[1 + t],
        device_id=(0, after),
        device_id_type=MESH,
    )
    to_before = pltpu.make_async_remote_copy(
        src_ref=scaled_ref.at[pl.ds(0, HALO)],
        dst_ref=win.at[t, pl.ds(span, HALO)],
        send_sem=send_halo.at[2],
        recv_sem=recv_halo.at[1 + t],
        device_id=(1, before),
        device_id_type=MESH,
    )
    to_peer.start()
    to_after.start()
    to_before.start()
    station_copies = []
    for d in range(1, space):
        copy = pltpu.make_async_remote_copy(
            src_ref=pack_ref,
            dst_ref=sta.at[d],
            send_sem=send_sta.at[d],
            recv_sem=recv_sta.at[d],
            device_id=(t, lax.rem(s + d, space)),
            device_id_type=MESH,
        )
        copy.start()
        station_copies.append(copy)
    sta[0] = pack_ref[...]
    win[t, pl.ds(HALO * (1 - t), span)] = scaled_ref[pl.ds(HALO * t, span)]

    def landed(dst, sem):
        pltpu.make_async_copy(dst, dst, sem).wait()

    landed(win.at[peer, pl.ds(HALO * peer, span)], recv_halo.at[0])
    edge = span * t
    landed(win.at[0, pl.ds(edge, HALO)], recv_halo.at[1])
    landed(win.at[1, pl.ds(edge, HALO)], recv_halo.at[2])

    rows = half + 2 * HALO
    bias = jnp.broadcast_to(bias_ref[...], (hidden, width))
    gain = jnp.broadcast_to(gain_ref[...], (hidden, width))

    def products(weight_ref, columns, count):
        outs = weight_ref.shape[0]
        for r in range(count):
            prod[r, :outs] = jnp.dot(
                weight_ref[...], columns[r], preferred_element_type=jnp.float32
            )

    def summed(y, outs):
        return (
            prod[y, 0:outs] + prod[y + 1, outs : 2 * outs] + prod[y + 2, 2 * outs : 3 * outs]
        )

    for r in range(rows):
        both = jnp.concatenate(
            [win[0, r].astype(jnp.float32), win[1, r].astype(jnp.float32)], axis=0
        )
        cols_in[r] = with_neighbours(both)
    products(w_in_ref, cols_in, rows)
    for y in range(rows - 2):
        value = gate(summed(y, hidden) + bias)
        first[y] = value.astype(jnp.bfloat16)
        cols_hid[y] = with_neighbours(value)
    products(w_mid_ref, cols_hid, rows - 2)
    for y in range(rows - 4):
        middle = summed(y, hidden)
        power = jnp.mean(middle * middle, axis=0, keepdims=True)
        cols_sec[y] = with_neighbours(gate(middle * lax.rsqrt(power + 1e-05) * gain))
    products(w_res_ref, cols_sec, rows - 4)
    for y in range(rows - 6):
        value = first[y + 2].astype(jnp.float32) + gate(summed(y, hidden))
        cols_third[y] = with_neighbours(value)
    products(w_out_ref, cols_third, rows - 6)
    for y in range(half):
        value = summed(y, 2 * chans)
        result[0, y] = value[:chans]
        result[1, y] = value[chans:]

    to_other = pltpu.make_async_remote_copy(
        src_ref=result.at[peer],
        dst_ref=arrived,
        send_sem=send_out,
        recv_sem=recv_out,
        device_id=(peer, s),
        device_id_type=MESH,
    )
    to_other.start()

    for copy in station_copies:
        copy.wait()
    lanes = pack_ref.shape[1]
    row_iota = lax.broadcasted_iota(jnp.int32, (strip, lanes), 0).astype(jnp.float32)
    col_iota = lax.broadcasted_iota(jnp.int32, (width, lanes), 0).astype(jnp.float32)
    top = (s * strip).astype(jnp.float32)
    terms = chans + 1
    for d in range(space):
        block = sta[d]
        at_row = jnp.where(row_iota == block[terms : terms + 1] - top, 1.0, 0.0)
        at_col = jnp.where(col_iota == block[terms + 1 : terms + 2], 1.0, 0.0)
        right_hand[:, d * lanes : (d + 1) * lanes] = at_col.astype(jnp.bfloat16)
        for k in range(terms):
            spread = block[k : k + 1] * at_row
            coarse = spread.astype(jnp.bfloat16)
            fine = (spread - coarse.astype(jnp.float32)).astype(jnp.bfloat16)
            left_hand[k * strip : (k + 1) * strip, d * lanes : (d + 1) * lanes] = coarse
            left_hand[
                (terms + k) * strip : (terms + k + 1) * strip, d * lanes : (d + 1) * lanes
            ] = fine
    placed = lax.dot_general(
        left_hand[...],
        right_hand[...],
        (((1,), (1,)), ((), ())),
        preferred_element_type=jnp.float32,
    )
    pull_ref[...] = placed[: terms * strip] + placed[terms * strip :]

    den_ref[pl.ds(half * t, half)] = result[t]
    to_peer.wait_send()
    to_after.wait_send()
    to_before.wait_send()
    to_other.wait()
    den_ref[pl.ds(half * peer, half)] = arrived[...]


def local_fused(
    noisy_state,
    fresh_noise,
    level_index,
    station_obs,
    obs_variance,
    station_owner,
    station_cell,
    conv_in,
    conv_mid,
    conv_res,
    conv_out,
    in_bias,
    noise_embed,
    norm_gain,
):
    steps, layers, strip, width = noisy_state.shape
    chans = steps * layers
    hidden = in_bias.shape[0]
    space = lax.axis_size("space")
    count = station_cell.shape[0]
    noise_scale = scale_at(level_index[0])
    next_scale = scale_at(level_index[0] - 1)
    bias = in_bias + noise_embed * jnp.log(10.0 * noise_scale)
    scaled = (noisy_state / jnp.sqrt(1.0 + noise_scale * noise_scale)).astype(jnp.bfloat16)
    scaled = scaled.reshape(chans, strip, width).transpose(1, 0, 2)
    weight = 1.0 / (obs_variance + noise_scale * noise_scale)
    where_row = station_owner[:, 0] * strip + station_cell // width
    where_col = station_cell % width
    terms = chans + 1
    packed_rows = -(-(terms + 2) // 8) * 8
    pack = jnp.concatenate(
        [
            station_obs.reshape(chans, count) * weight[None],
            weight[None],
            where_row.astype(jnp.float32)[None],
            where_col.astype(jnp.float32)[None],
            jnp.zeros((packed_rows - terms - 2, count), jnp.float32),
        ],
        axis=0,
    )
    half = strip // 2
    rows = half + 2 * HALO
    vmem = pl.BlockSpec(memory_space=pltpu.VMEM)
    den, pull = pl.pallas_call(
        lambda *refs: fused_kernel(space, *refs),
        out_shape=(
            jax.ShapeDtypeStruct((strip, chans, width), jnp.float32),
            jax.ShapeDtypeStruct((terms * strip, width), jnp.float32),
        ),
        in_specs=[vmem] * 8,
        out_specs=(vmem, vmem),
        scratch_shapes=[
            pltpu.VMEM((2, rows, chans, width), jnp.bfloat16),
            pltpu.VMEM((space, packed_rows, count), jnp.float32),
            pltpu.VMEM((rows, 6 * chans, width), jnp.bfloat16),
            pltpu.VMEM((rows - 2, 3 * hidden, width), jnp.bfloat16),
            pltpu.VMEM((rows - 4, 3 * hidden, width), jnp.bfloat16),
            pltpu.VMEM((rows - 6, 3 * hidden, width), jnp.bfloat16),
            pltpu.VMEM((rows, 3 * hidden, width), jnp.float32),
            pltpu.VMEM((rows - 2, hidden, width), jnp.bfloat16),
            pltpu.VMEM((2, half, chans, width), jnp.float32),
            pltpu.VMEM((half, chans, width), jnp.float32),
            pltpu.VMEM((2 * terms * strip, space * count), jnp.bfloat16),
            pltpu.VMEM((width, space * count), jnp.bfloat16),
            pltpu.SemaphoreType.DMA((3,)),
            pltpu.SemaphoreType.DMA((3,)),
            pltpu.SemaphoreType.DMA((space,)),
            pltpu.SemaphoreType.DMA((space,)),
            pltpu.SemaphoreType.DMA,
            pltpu.SemaphoreType.DMA,
        ],
        compiler_params=pltpu.CompilerParams(
            collective_id=0, has_side_effects=True, vmem_limit_bytes=40 * 1024 * 1024
        ),
        name="score_and_stations",
    )(
        scaled,
        pack,
        conv_in.reshape(-1, conv_in.shape[2]),
        conv_mid.reshape(-1, conv_mid.shape[2]),
        conv_res.reshape(-1, conv_res.shape[2]),
        conv_out.reshape(-1, conv_out.shape[2]),
        bias[:, None],
        norm_gain[:, None],
    )
    window_out = den.transpose(1, 0, 2).reshape(noisy_state.shape)
    estimate = noisy_state - noise_scale * window_out
    pull = pull.reshape(terms, strip, width)
    observed = pull[:chans].reshape(noisy_state.shape)
    total = observed - estimate * pull[chans]
    return estimate + noise_scale * noise_scale * total + next_scale * fresh_noise


def solution(mesh):
    placed = (
        P("tm", None, "space", None),
        P("tm", None, "space", None),
        P(),
        P("tm", None, "space"),
        P("space"),
        P("space", None),
        P("space"),
        P(),
        P(),
        P(),
        P(),
        P(),
        P(),
        P(),
    )
    pair = mesh.shape["tm"] == 2
    return jax.shard_map(
        local_fused if pair else local, mesh=mesh, in_specs=placed, out_specs=P("tm", None, "space", None), check_vma=False
    )
```

```python
import jax
import jax.numpy as jnp
from jax import lax
from jax.experimental import pallas as pl
from jax.experimental.pallas import tpu as pltpu
from jax.sharding import PartitionSpec as P

WIN = 8
LEVELS = 32
STRIDE = 4
CHAN = 16


def extended_2(cells, sides, width):
    for axis, dim in sides:
        count = lax.axis_size(axis)
        head = lax.slice_in_dim(cells, 0, width, axis=dim)
        tail = lax.slice_in_dim(cells, cells.shape[dim] - width, cells.shape[dim], axis=dim)
        cells = jnp.concatenate(
            [
                lax.ppermute(tail, axis, [(i, (i + 1) % count) for i in range(count)]),
                cells,
                lax.ppermute(head, axis, [((i + 1) % count, i) for i in range(count)]),
            ],
            axis=dim,
        )
    return cells


def shifted(value, axis, steps):
    count = lax.axis_size(axis)
    first, last = (max(0, -steps), min(count, count - steps))
    return lax.ppermute(value, axis, [(source, source + steps) for source in range(first, last)])


def scale_at(level):
    return 0.3 * jnp.exp(jnp.log(5.0) * level.astype(jnp.float32) / (LEVELS - 1))


def conv_rows(weight, padded):
    out_rows = padded.shape[2] - 2
    stacked = jnp.concatenate(
        [jnp.roll(padded, 1 - col_tap, axis=3) for col_tap in range(3)], axis=1
    )
    total = None
    for row_tap in range(3):
        product = jnp.einsum(
            "oc,ncyx->noyx",
            weight[row_tap],
            stacked[:, :, row_tap : row_tap + out_rows, :],
            preferred_element_type=jnp.float32,
        )
        total = product if total is None else total + product
    return total


def hidden_rim(hidden):
    return extended_2(hidden, (("space", 2),), 1)


def score_net(windows, conv_in, conv_mid, conv_res, conv_out, bias, norm_gain):
    source = extended_2(windows, (("space", 2),), 1)
    first = jax.nn.silu(conv_rows(conv_in, source) + bias[None, :, None, None]).astype(jnp.bfloat16)
    middle = conv_rows(conv_mid, hidden_rim(first))
    normed = (
        middle
        * lax.rsqrt(jnp.mean(middle * middle, axis=1, keepdims=True) + 1e-05)
        * norm_gain[None, :, None, None]
    )
    second = jax.nn.silu(normed).astype(jnp.bfloat16)
    branch = jax.nn.silu(conv_rows(conv_res, hidden_rim(second)))
    third = (first.astype(jnp.float32) + branch).astype(jnp.bfloat16)
    return conv_rows(conv_out, hidden_rim(third))


def local(
    noisy_state,
    fresh_noise,
    level_index,
    station_obs,
    obs_variance,
    station_owner,
    station_cell,
    conv_in,
    conv_mid,
    conv_res,
    conv_out,
    in_bias,
    noise_embed,
    norm_gain,
):
    step_count, layer_count, row_count, col_count = noisy_state.shape
    noise_scale = scale_at(level_index[0])
    next_scale = scale_at(level_index[0] - 1)
    bias = in_bias + noise_embed * jnp.log(10.0 * noise_scale)
    scaled = (noisy_state / jnp.sqrt(1.0 + noise_scale * noise_scale)).astype(jnp.bfloat16)
    time_rank = lax.axis_index("tm")
    total_steps = step_count * lax.axis_size("tm")
    ahead = shifted(scaled, "tm", -1)
    extended = jnp.concatenate([scaled, ahead], axis=0)
    offset = 0
    window_count = (extended.shape[0] - WIN) // STRIDE + 1
    windows = jnp.stack([extended])
    windows = windows.reshape(window_count, CHAN, row_count, col_count)
    outputs = score_net(windows, conv_in, conv_mid, conv_res, conv_out, bias, norm_gain)
    starts = time_rank * step_count - offset + STRIDE * jnp.arange(window_count, dtype=jnp.int32)
    usable = ((starts >= 0) & (starts + WIN <= total_steps)).astype(jnp.float32)
    halves = (
        outputs.reshape(window_count, 2, STRIDE, layer_count, row_count, col_count)
        * usable[:, None, None, None, None, None]
    )
    blank = jnp.zeros((1, STRIDE, layer_count, row_count, col_count), jnp.float32)
    summed = jnp.concatenate([halves[:, 0], blank], axis=0) + jnp.concatenate(
        [blank, halves[:, 1]], axis=0
    )
    summed = summed.reshape(extended.shape[0], layer_count, row_count, col_count)
    spill = shifted(summed[step_count:], "tm", 1)
    own = jnp.concatenate([summed[:STRIDE] + spill, summed[STRIDE:step_count]], axis=0)
    moment = time_rank * step_count + jnp.arange(step_count, dtype=jnp.int32)
    cover = jnp.where((moment < STRIDE) | (moment >= total_steps - STRIDE), 1.0, 2.0).astype(
        jnp.float32
    )
    estimate = noisy_state - noise_scale * (own / cover[:, None, None, None])
    space_size = lax.axis_size("space")
    station_count = station_cell.shape[0]
    capacity = 4 * station_count // space_size
    values = station_obs.reshape(step_count * layer_count, station_count)
    target = station_owner[:, 0]
    earlier = lax.broadcasted_iota(
        jnp.int32, (station_count, station_count), 0
    ) < lax.broadcasted_iota(jnp.int32, (station_count, station_count), 1)
    ranked = jnp.sum(
        jnp.where((target[:, None] == target[None, :]) & earlier, 1, 0), axis=0
    ).astype(jnp.int32)
    slot = target * capacity + ranked
    slot_count = space_size * capacity
    value_slots = jnp.zeros((values.shape[0], slot_count), jnp.float32).at[:, slot].set(values)
    spread_slots = jnp.zeros((1, slot_count), jnp.float32).at[0, slot].set(obs_variance)
    cell_slots = jnp.full((1, slot_count), -1, jnp.int32).at[0, slot].set(station_cell)
    got_values, got_spread, got_cells = (
        lax.all_to_all(value_slots, "space", split_axis=1, concat_axis=1, tiled=True),
        lax.all_to_all(spread_slots, "space", split_axis=1, concat_axis=1, tiled=True),
        lax.all_to_all(cell_slots, "space", split_axis=1, concat_axis=1, tiled=True),
    )
    present = got_cells[0] >= 0
    spot = jnp.maximum(got_cells[0], 0)
    flat = estimate.reshape(step_count * layer_count, row_count * col_count)
    seen = jnp.take(flat, spot, axis=1)
    misfit = jnp.where(
        present[None, :], (got_values - seen) / (got_spread + noise_scale * noise_scale), 0.0
    )
    pull = jnp.zeros_like(flat).at[:, spot].add(misfit)
    return (
        estimate
        + noise_scale * noise_scale * pull.reshape(estimate.shape)
        + next_scale * fresh_noise
    )


MESH = pl.DeviceIdType.MESH
HALO = 4


def gate(v):
    return 0.5 * v * (jnp.tanh(0.5 * v) + 1.0)


def with_neighbours(v):
    cols = v.shape[1]
    return jnp.concatenate(
        [pltpu.roll(v, 1, axis=1), v, pltpu.roll(v, cols - 1, axis=1)], axis=0
    ).astype(jnp.bfloat16)


def fused_kernel(
    space,
    level_ref,
    noisy_hbm,
    fresh_hbm,
    obs_ref,
    variance_ref,
    owner_ref,
    cell_ref,
    w_in_ref,
    w_mid_hbm,
    w_res_hbm,
    w_out_hbm,
    bias_ref,
    embed_ref,
    gain_ref,
    next_ref,
    noisy_ref,
    fresh_ref,
    w_in_rows,
    w_mid_ref,
    w_res_ref,
    w_out_ref,
    load_sem,
    scaled_ref,
    pack_ref,
    win,
    sta,
    cols_in,
    cols_hid,
    cols_sec,
    cols_third,
    prod,
    first,
    result,
    arrived,
    whole,
    pulls,
    left_hand,
    right_hand,
    send_halo,
    recv_halo,
    send_sta,
    recv_sta,
    send_out,
    recv_out,
):
    t = lax.axis_index("tm")
    s = lax.axis_index("space")
    peer = 1 - t
    after = lax.rem(s + 1, space)
    before = lax.rem(s + space - 1, space)
    diagonal = lax.rem(s + space - 1 + 2 * t, space)
    chans, strip, width = noisy_ref.shape
    half = strip // 2
    span = half + HALO
    hidden = bias_ref.shape[1]
    count = cell_ref.shape[1]

    loads = [
        pltpu.make_async_copy(source, target, load_sem.at[k])
        for k, (source, target) in enumerate(
            (
                (noisy_hbm, noisy_ref),
                (w_mid_hbm, w_mid_ref),
                (w_res_hbm, w_res_ref),
                (w_out_hbm, w_out_ref),
                (fresh_hbm, fresh_ref),
            )
        )
    ]
    for load in loads:
        load.start()
    barrier = pltpu.get_barrier_semaphore()
    pl.semaphore_signal(barrier, inc=1, device_id=(peer, s), device_id_type=MESH)
    pl.semaphore_signal(barrier, inc=1, device_id=(peer, diagonal), device_id_type=MESH)
    for d in range(1, space):
        pl.semaphore_signal(
            barrier, inc=1, device_id=(t, lax.rem(s + d, space)), device_id_type=MESH
        )

    noise = scale_at(jnp.full((1, width), level_ref[0], jnp.int32))
    following = scale_at(jnp.full((1, width), level_ref[0] - 1, jnp.int32))
    spread_out = jnp.sqrt(1.0 + noise * noise)
    loads[0].wait()
    for y in range(strip):
        scaled_ref[y] = (noisy_ref[:, y, :] / spread_out).astype(jnp.bfloat16)
    noise_sta = noise[:, :1]
    weight = 1.0 / (variance_ref[...] + noise_sta * noise_sta)
    cell = cell_ref[...].astype(jnp.float32)
    cell_row = jnp.floor((cell + 0.5) / width)
    sort = lax.broadcasted_iota(jnp.int32, (8, count), 0)
    pack_ref[0:chans] = obs_ref[...] * weight
    pack_ref[chans : chans + 8] = jnp.where(
        sort == 0,
        weight,
        jnp.where(
            sort == 1,
            owner_ref[...].astype(jnp.float32) * strip + cell_row,
            jnp.where(sort == 2, cell - cell_row * width, 0.0),
        ),
    )
    pl.semaphore_wait(barrier, space + 1)

    to_peer = pltpu.make_async_remote_copy(
        src_ref=scaled_ref.at[pl.ds(HALO * peer, span)],
        dst_ref=win.at[t, pl.ds(HALO * t, span)],
        send_sem=send_halo.at[0],
        recv_sem=recv_halo.at[0],
        device_id=(peer, s),
        device_id_type=MESH,
    )
    to_after = pltpu.make_async_remote_copy(
        src_ref=scaled_ref.at[pl.ds(strip - HALO, HALO)],
        dst_ref=win.at[t, pl.ds(0, HALO)],
        send_sem=send_halo.at[1],
        recv_sem=recv_halo.at[1 + t],
        device_id=(0, after),
        device_id_type=MESH,
    )
    to_before = pltpu.make_async_remote_copy(
        src_ref=scaled_ref.at[pl.ds(0, HALO)],
        dst_ref=win.at[t, pl.ds(span, HALO)],
        send_sem=send_halo.at[2],
        recv_sem=recv_halo.at[1 + t],
        device_id=(1, before),
        device_id_type=MESH,
    )
    to_peer.start()
    to_after.start()
    to_before.start()
    station_copies = []
    for d in range(1, space):
        copy = pltpu.make_async_remote_copy(
            src_ref=pack_ref,
            dst_ref=sta.at[d],
            send_sem=send_sta.at[d],
            recv_sem=recv_sta.at[d],
            device_id=(t, lax.rem(s + d, space)),
            device_id_type=MESH,
        )
        copy.start()
        station_copies.append(copy)
    sta[0] = pack_ref[...]
    win[t, pl.ds(HALO * (1 - t), span)] = scaled_ref[pl.ds(HALO * t, span)]

    for tap in range(3):
        w_in_rows[hidden * tap : hidden * (tap + 1)] = (
            w_in_ref[tap].astype(jnp.float32).T.astype(jnp.bfloat16)
        )
    for load in loads[1:4]:
        load.wait()

    def landed(dst, sem):
        pltpu.make_async_copy(dst, dst, sem).wait()

    landed(win.at[peer, pl.ds(HALO * peer, span)], recv_halo.at[0])
    edge = span * t
    landed(win.at[0, pl.ds(edge, HALO)], recv_halo.at[1])
    landed(win.at[1, pl.ds(edge, HALO)], recv_halo.at[2])

    rows = half + 2 * HALO
    shift = jnp.log(10.0 * noise)[:, :hidden]
    bias = jnp.broadcast_to(bias_ref[...] + embed_ref[...] * shift, (width, hidden)).T
    gain = jnp.broadcast_to(gain_ref[...], (width, hidden)).T

    def products(weight_ref, columns, count):
        outs = weight_ref.shape[0]
        for r in range(count):
            prod[r, :outs] = jnp.dot(
                weight_ref[...], columns[r], preferred_element_type=jnp.float32
            )

    def summed(y, outs):
        return (
            prod[y, 0:outs] + prod[y + 1, outs : 2 * outs] + prod[y + 2, 2 * outs : 3 * outs]
        )

    for r in range(rows):
        both = jnp.concatenate(
            [win[0, r].astype(jnp.float32), win[1, r].astype(jnp.float32)], axis=0
        )
        cols_in[r] = with_neighbours(both)
    products(w_in_rows, cols_in, rows)
    for y in range(rows - 2):
        value = gate(summed(y, hidden) + bias)
        first[y] = value.astype(jnp.bfloat16)
        cols_hid[y] = with_neighbours(value)
    products(w_mid_ref, cols_hid, rows - 2)
    for y in range(rows - 4):
        middle = summed(y, hidden)
        power = jnp.mean(middle * middle, axis=0, keepdims=True)
        cols_sec[y] = with_neighbours(gate(middle * lax.rsqrt(power + 1e-05) * gain))
    products(w_res_ref, cols_sec, rows - 4)
    for y in range(rows - 6):
        value = first[y + 2].astype(jnp.float32) + gate(summed(y, hidden))
        cols_third[y] = with_neighbours(value)
    products(w_out_ref, cols_third, rows - 6)
    for y in range(half):
        value = summed(y, 2 * chans)
        result[0, y] = value[:chans]
        result[1, y] = value[chans:]

    to_other = pltpu.make_async_remote_copy(
        src_ref=result.at[peer],
        dst_ref=arrived,
        send_sem=send_out,
        recv_sem=recv_out,
        device_id=(peer, s),
        device_id_type=MESH,
    )
    to_other.start()

    for copy in station_copies:
        copy.wait()
    lanes = pack_ref.shape[1]
    row_iota = lax.broadcasted_iota(jnp.int32, (strip, lanes), 0).astype(jnp.float32)
    col_iota = lax.broadcasted_iota(jnp.int32, (width, lanes), 0).astype(jnp.float32)
    top = (s * strip).astype(jnp.float32)
    terms = chans + 1
    for d in range(space):
        block = sta[d]
        at_row = jnp.where(row_iota == block[terms : terms + 1] - top, 1.0, 0.0)
        at_col = jnp.where(col_iota == block[terms + 1 : terms + 2], 1.0, 0.0)
        right_hand[:, d * lanes : (d + 1) * lanes] = at_col.astype(jnp.bfloat16)
        span_of = slice(d * lanes, (d + 1) * lanes)

        def put(at, spread):
            coarse = spread.astype(jnp.bfloat16)
            fine = (spread - coarse.astype(jnp.float32)).astype(jnp.bfloat16)
            left_hand[at : at + spread.shape[0], span_of] = coarse
            at = terms * strip + at
            left_hand[at : at + spread.shape[0], span_of] = fine

        for y in range(0, strip, 2):
            put(
                chans * y,
                jnp.concatenate(
                    [block[:chans] * at_row[y : y + 1], block[:chans] * at_row[y + 1 : y + 2]],
                    axis=0,
                ),
            )
        put(chans * strip, block[chans : chans + 1] * at_row)
    placed = lax.dot_general(
        left_hand[...],
        right_hand[...],
        (((1,), (1,)), ((), ())),
        preferred_element_type=jnp.float32,
    )
    pulls[...] = placed[: terms * strip] + placed[terms * strip :]
    to_peer.wait_send()
    to_after.wait_send()
    to_before.wait_send()
    to_other.wait()
    whole[pl.ds(half * t, half)] = result[t]
    whole[pl.ds(half * peer, half)] = arrived[...]
    loads[4].wait()
    for y in range(strip):
        estimate = noisy_ref[:, y, :] - noise * whole[y]
        base = chans * strip + y
        pull = pulls[chans * y : chans * (y + 1)] - estimate * pulls[base : base + 1]
        next_ref[y] = estimate + noise * noise * pull + following * fresh_ref[:, y, :]


def local_fused(
    noisy_state,
    fresh_noise,
    level_index,
    station_obs,
    obs_variance,
    station_owner,
    station_cell,
    conv_in,
    conv_mid,
    conv_res,
    conv_out,
    in_bias,
    noise_embed,
    norm_gain,
):
    steps, layers, strip, width = noisy_state.shape
    chans = steps * layers
    hidden = in_bias.shape[0]
    space = lax.axis_size("space")
    count = station_cell.shape[0]
    terms = chans + 1
    packed_rows = chans + 8
    half = strip // 2
    rows = half + 2 * HALO
    hbm = pl.BlockSpec(memory_space=pltpu.MemorySpace.HBM)
    vmem = pl.BlockSpec(memory_space=pltpu.VMEM)
    result = pl.pallas_call(
        lambda *refs: fused_kernel(space, *refs),
        out_shape=jax.ShapeDtypeStruct((strip, chans, width), jnp.float32),
        in_specs=[pl.BlockSpec(memory_space=pltpu.SMEM), hbm, hbm]
        + [vmem] * 5
        + [hbm] * 3
        + [vmem] * 3,
        out_specs=vmem,
        scratch_shapes=[
            pltpu.VMEM((chans, strip, width), jnp.float32),
            pltpu.VMEM((chans, strip, width), jnp.float32),
            pltpu.VMEM((3 * hidden, conv_in.shape[2]), jnp.bfloat16),
            pltpu.VMEM((3 * hidden, 3 * hidden), jnp.bfloat16),
            pltpu.VMEM((3 * hidden, 3 * hidden), jnp.bfloat16),
            pltpu.VMEM((6 * chans, 3 * hidden), jnp.bfloat16),
            pltpu.SemaphoreType.DMA((5,)),
            pltpu.VMEM((strip, chans, width), jnp.bfloat16),
            pltpu.VMEM((packed_rows, count), jnp.float32),
            pltpu.VMEM((2, rows, chans, width), jnp.bfloat16),
            pltpu.VMEM((space, packed_rows, count), jnp.float32),
            pltpu.VMEM((rows, 6 * chans, width), jnp.bfloat16),
            pltpu.VMEM((rows - 2, 3 * hidden, width), jnp.bfloat16),
            pltpu.VMEM((rows - 4, 3 * hidden, width), jnp.bfloat16),
            pltpu.VMEM((rows - 6, 3 * hidden, width), jnp.bfloat16),
            pltpu.VMEM((rows, 3 * hidden, width), jnp.float32),
            pltpu.VMEM((rows - 2, hidden, width), jnp.bfloat16),
            pltpu.VMEM((2, half, chans, width), jnp.float32),
            pltpu.VMEM((half, chans, width), jnp.float32),
            pltpu.VMEM((strip, chans, width), jnp.float32),
            pltpu.VMEM((terms * strip, width), jnp.float32),
            pltpu.VMEM((2 * terms * strip, space * count), jnp.bfloat16),
            pltpu.VMEM((width, space * count), jnp.bfloat16),
            pltpu.SemaphoreType.DMA((3,)),
            pltpu.SemaphoreType.DMA((3,)),
            pltpu.SemaphoreType.DMA((space,)),
            pltpu.SemaphoreType.DMA((space,)),
            pltpu.SemaphoreType.DMA,
            pltpu.SemaphoreType.DMA,
        ],
        compiler_params=pltpu.CompilerParams(
            collective_id=0, has_side_effects=True
        ),
        name="score_and_stations",
    )(
        level_index,
        noisy_state.reshape(chans, strip, width),
        fresh_noise.reshape(chans, strip, width),
        station_obs.reshape(chans, count),
        obs_variance[None],
        station_owner.reshape(1, count),
        station_cell[None],
        conv_in.transpose(0, 2, 1),
        conv_mid.reshape(-1, conv_mid.shape[2]),
        conv_res.reshape(-1, conv_res.shape[2]),
        conv_out.reshape(-1, conv_out.shape[2]),
        in_bias[None],
        noise_embed[None],
        norm_gain[None],
    )
    return result.transpose(1, 0, 2).reshape(noisy_state.shape)


def solution(mesh):
    placed = (
        P("tm", None, "space", None),
        P("tm", None, "space", None),
        P(),
        P("tm", None, "space"),
        P("space"),
        P("space", None),
        P("space"),
        P(),
        P(),
        P(),
        P(),
        P(),
        P(),
        P(),
    )
    pair = mesh.shape["tm"] == 2
    return jax.shard_map(
        local_fused if pair else local, mesh=mesh, in_specs=placed, out_specs=P("tm", None, "space", None), check_vma=False
    )
```
